128 devices in a mesh: seq: 32 (over x, y, core), head: 4 (over z).
Axes of the slice: x: 4, y: 4, z: 4, core: 2. Of those that a mesh axis runs over, the one named last changes fastest.
Arguments:
- queries: bfloat16 [65536, 4096], P('seq', 'head'), may hold values from -2 to 2
- key_rows: bfloat16 [65536, 4096], P('seq', 'head'), may hold values from -2 to 2
- value_rows: bfloat16 [65536, 4096], P('seq', 'head'), may hold values from -128 to 128
- decay_log: float32 [32, 65536], P('head', 'seq'), may hold values from -0.8 to 0
- norm_gain: float32 [4096], P('head'), may hold values from 0.1 to 1.9
- page_owner: int32 [64], replicated, may hold values from 0 to 31, as said below
Outputs:
- attended: bfloat16 [65536, 4096], P('seq', 'head')
- page_cache: bfloat16 [160, 32, 128, 128], P('seq', 'head')
The draws below stay inside these ranges and needn't reach their ends.
Inputs may be any that keep to these rules, and one draw needn't show every extreme that they name: `page_owner`: the 2 pages p = i * 2 to (i + 1) * 2 - 1 have different owners for every i; no owner keeps more than 5 pages and one keeps exactly 5.
All inputs are finite; a program needn't handle non-finite values.
Results may differ from the reference program's by a relative error of at most 0.0042.
Values may be sent and summed in bfloat16 or wider, within the bound.
A program may use at most 128 MiB of HBM per device.

```python
import math
import jax
import jax.numpy as jnp
from jax import lax

HDIM = 128
TOK_DEV = 2048
BLOCK = 512
PAGE = 1024
SLOTS = 5
HEADS = 32
TOKENS = 65536
PAGES_DEV = 2
PAGES = 64
CACHE_ROWS = 160


def draw_value_rows(key, part):
    first, second, third = jax.random.split(key, 3)
    heads_rank = jnp.arange(HEADS).astype(jnp.float32)
    base = jnp.clip(jax.random.normal(first, (TOKENS, HEADS, HDIM), jnp.float32), -4.0, 4.0)
    head_scale = 10.0 ** ((heads_rank + jax.random.uniform(second, (HEADS,), jnp.float32)) / HEADS)
    row_scale = 10.0 ** (0.5 * jax.random.uniform(third, (TOKENS, 1, 1), jnp.float32))
    return (base * head_scale[None, :, None] * row_scale).reshape(TOKENS, HEADS * HDIM).astype(jnp.bfloat16)


def draw_decay_log(key, part):
    every_key_row = jax.random.split(key, 7)
    fast_share = 0.5
    fast = jax.random.uniform(every_key_row[0], (HEADS, 1), jnp.float32) < fast_share
    fast_rate = jax.random.uniform(every_key_row[1], (HEADS, 1), jnp.float32, 1.0 / 50.0, 1.0 / 30.0)
    slow_rate = jax.random.uniform(every_key_row[2], (HEADS, 1), jnp.float32, 0.1, 0.4) / TOKENS
    decay_rate = jnp.where(fast, fast_rate, slow_rate)
    segments = TOKENS // TOK_DEV
    decay_multiplier = jnp.exp(jax.random.uniform(every_key_row[3], (HEADS, segments), jnp.float32, math.log(0.5), math.log(2.0)))
    decay_multiplier = jnp.repeat(decay_multiplier, TOK_DEV, axis=1)
    leading_location = jax.random.randint(every_key_row[4], (), 0, TOKENS)
    trailing_location = (leading_location + 1 + jax.random.randint(every_key_row[6], (), 0, TOKENS - 1)) % TOKENS
    spike_location = jnp.stack([leading_location, trailing_location])
    spike_depth = jax.random.uniform(every_key_row[5], (2,), jnp.float32, math.log(1.25), math.log(2.0))
    token_positions = jnp.arange(TOKENS)
    spike_events = jnp.sum(jnp.where(token_positions[None, :] == spike_location[:, None], spike_depth[:, None], 0.0), axis=0)
    return -(decay_rate * decay_multiplier + spike_events[None, :])


def draw_page_owner(key, part):
    first, second, third, fourth = jax.random.split(key, 4)
    owner_count = PAGES // PAGES_DEV
    hottest = jax.random.randint(first, (), 0, owner_count)
    ranking = jax.random.permutation(second, owner_count)
    hot_device = ranking < SLOTS
    hot_page = jax.random.randint(third, (owner_count,), 0, PAGES_DEV)
    offset = jax.random.randint(fourth, (), 0, owner_count - 1)
    device_ids = jnp.arange(owner_count)[:, None]
    page_ids = jnp.arange(PAGES_DEV)[None, :]
    others = (hottest + 1 + (device_ids + page_ids + offset) % (owner_count - 1)) % owner_count
    chosen = jnp.where(hot_device[:, None] & (page_ids == hot_page[:, None]), hottest, others)
    return chosen.reshape(PAGES).astype(jnp.int32)


def steps_of(rng, dims, shards, low, top_value):
    level, own = 1.0, jax.random.fold_in(rng, 6)
    for position, shards_of in shards:
        steps = jnp.exp(jax.random.uniform(jax.random.fold_in(own, position), (shards_of,), jnp.float32, low / len(shards), top_value / len(shards)))
        level = level * jnp.repeat(steps, dims[position] // shards_of).reshape([-1 if axis == position else 1 for axis in range(len(dims))])
    return level


def normal_values(rng, shape, width, reach, shards=(), dtype=jnp.bfloat16):
    array = width * jax.random.normal(rng, shape, jnp.float32)
    if shards:
        array = array * steps_of(rng, shape, shards, -0.22, 0.18)
    return jnp.clip(array, -reach, reach).astype(dtype)


def setup_inputs(seed: int = 0) -> dict:
    splits = jax.random.split(jax.random.key(seed), 7)
    queries = normal_values(splits[0], (TOKENS, HEADS * HDIM), 0.3, 2.0, ((0, 32), (1, 4)))
    key_rows = normal_values(splits[1], (TOKENS, HEADS * HDIM), 0.3, 2.0, ((0, 32), (1, 4)))
    value_rows = draw_value_rows(jax.random.fold_in(splits[6], 71), 0)
    decay_log = draw_decay_log(jax.random.fold_in(splits[6], 71), 0)
    norm_gain = jnp.clip(1.0 + 0.18 * jax.random.normal(splits[4], (HEADS * HDIM,), jnp.float32), 0.1, 1.9)
    page_owner = draw_page_owner(jax.random.fold_in(splits[6], 71), 0)
    return {"queries": queries, "key_rows": key_rows, "value_rows": value_rows, "decay_log": decay_log, "norm_gain": norm_gain, "page_owner": page_owner}


def block_terms(query_blk, key_blk, value_blk, cumulative, carry_state):
    length = cumulative.shape[1]
    token_positions = jnp.arange(length)
    causal = (token_positions[:, None] >= token_positions[None, :])[None]
    spread = cumulative[:, :, None] - cumulative[:, None, :]
    damping = jnp.where(causal, jnp.exp(jnp.where(causal, spread, 0.0)), 0.0)
    scores = jnp.einsum('thd,shd->hts', query_blk.astype(jnp.float32), key_blk.astype(jnp.float32))
    weights = (scores * damping).astype(jnp.bfloat16)
    inner_sum = jnp.einsum('hts,shd->thd', weights.astype(jnp.float32), value_blk.astype(jnp.float32))
    carried = jnp.einsum('thd,hde->the', query_blk.astype(jnp.float32), carry_state, precision=lax.Precision.HIGHEST)
    output = inner_sum + carried * jnp.exp(cumulative).T[:, :, None]
    scaled_keys = (key_blk.astype(jnp.float32) * jnp.exp(cumulative[:, -1:] - cumulative).T[:, :, None]).astype(jnp.bfloat16)
    update = jnp.einsum('shd,she->hde', scaled_keys.astype(jnp.float32), value_blk.astype(jnp.float32))
    new_state = jnp.exp(cumulative[:, -1])[:, None, None] * carry_state + update
    return (output, new_state)

def reference(queries, key_rows, value_rows, decay_log, norm_gain, page_owner):
    per_page = PAGE // BLOCK
    block_shape = (PAGES, per_page, BLOCK, HEADS, HDIM)
    query_all = queries.reshape(block_shape)
    key_all = key_rows.reshape(block_shape)
    value_all = value_rows.reshape(block_shape)
    decay_all = decay_log.reshape(HEADS, PAGES, per_page, BLOCK).transpose(1, 2, 0, 3)
    gain_grid = norm_gain.reshape(HEADS, HDIM)

    def block_step(carry_state, pieces):
        query_blk, key_blk, value_blk, decay_blk = pieces
        cumulative = jnp.cumsum(decay_blk, axis=1)
        output, new_state = block_terms(query_blk, key_blk, value_blk, cumulative, carry_state)
        mean_square = lax.optimization_barrier(jnp.mean(output * output, axis=(1, 2)))
        normed = output * lax.rsqrt(mean_square + 1e-06)[:, None, None] * gain_grid[None]
        return (new_state, normed.astype(jnp.bfloat16).reshape(BLOCK, HEADS * HDIM))

    def page_step(carry_state, pieces):
        carry_state, normed = lax.scan(block_step, carry_state, pieces)
        return (carry_state, (normed, carry_state.astype(jnp.bfloat16)))
    initial = jnp.zeros((HEADS, HDIM, HDIM), jnp.float32)
    final_state, (normed, snapshots) = lax.scan(page_step, initial, (query_all, key_all, value_all, decay_all))
    attended = normed.reshape(TOKENS, HEADS * HDIM)
    page_order = jnp.arange(PAGES)
    earlier = (page_owner[:, None] == page_owner[None, :]) & (page_order[None, :] < page_order[:, None])
    slot_index = lax.optimization_barrier(jnp.sum(earlier.astype(jnp.int32), axis=1))
    target = (page_owner * SLOTS + slot_index).astype(jnp.int32)
    page_cache = jnp.zeros((CACHE_ROWS, HEADS, HDIM, HDIM), jnp.bfloat16).at[target].set(snapshots)
    return (attended, page_cache)
```

```python
import functools

import jax
import jax.numpy as jnp
from jax import lax
from jax.experimental import pallas as pl
from jax.experimental.pallas import tpu as pltpu
from jax.sharding import PartitionSpec as P

SLOTS = 5
HD = 128
HALF = 128
CHUNK = 256
LOG2E = 1.4426950408889634
BF = jnp.bfloat16
F32 = jnp.float32
MESH = pl.DeviceIdType.MESH
INTRA_EARLY = 4


def lanes_scan(x, lane):
    for shift in (1, 2, 4, 8, 16, 32, 64):
        x = x + jnp.where(lane >= shift, pltpu.roll(x, shift, axis=1), 0.0)
    return x


def three_parts(row, sub):
    x = jnp.broadcast_to(row, (8, 128))
    hi = x.astype(BF).astype(F32)
    rest = x - hi
    mid = rest.astype(BF).astype(F32)
    lo = rest - mid
    return jnp.where(sub == 0, hi, jnp.where(sub == 1, mid, jnp.where(sub == 2, lo, 0.0)))


def column_of(row):
    return jnp.broadcast_to(row, (HALF, HALF)).T


def kernel(
    n_seq,
    n_head,
    idx_ref,
    q_hbm,
    k_hbm,
    v_hbm,
    d_hbm,
    g_hbm,
    att_hbm,
    cache_hbm,
    qb,
    kb,
    vb,
    acc,
    ob,
    sl,
    up,
    en,
    d_ref,
    g_ref,
    c_ref,
    f_ref,
    a_ref,
    b_ref,
    pd_ref,
    sendbuf,
    recvbuf,
    snap,
    pagebuf,
    ent,
    sq_send,
    sq_recv,
    scale_ref,
    in_sem,
    q_sem,
    small_sem,
    a_send,
    a_recv,
    e_send,
    e_recv,
    p_send,
    p_recv,
    p_self,
    s_send,
    s_recv,
    o_sem,
):
    heads = kb.shape[0]
    toks = kb.shape[1]
    chunks = toks // CHUNK
    per_page = chunks // 2
    me = lax.axis_index("seq")
    z = lax.axis_index("head")
    parts = n_seq // heads
    rows = HD // parts
    g = me // parts
    r0 = pl.multiple_of((me % parts) * rows, rows)

    def kv_copies(step):
        h = (g + step) % heads
        hc = pl.multiple_of(h * HD, HD)
        return (
            pltpu.make_async_copy(k_hbm.at[:, pl.ds(hc, HD)], kb.at[h], in_sem.at[0, step]),
            pltpu.make_async_copy(v_hbm.at[:, pl.ds(hc, HD)], vb.at[h], in_sem.at[1, step]),
        )

    def q_copy(h):
        hc = pl.multiple_of(h * HD, HD)
        return pltpu.make_async_copy(q_hbm.at[:, pl.ds(hc, HD)], qb.at[h], q_sem.at[h])

    d_copy = pltpu.make_async_copy(d_hbm, d_ref, small_sem.at[0])
    g_copy = pltpu.make_async_copy(g_hbm, g_ref, small_sem.at[1])
    d_copy.start()

    @pl.loop(0, heads)
    def _(step):
        for copy in kv_copies(step):
            copy.start()

    @pl.loop(0, heads)
    def _(h):
        q_copy(h).start()

    g_copy.start()

    barrier = pltpu.get_barrier_semaphore()

    @pl.loop(1, n_seq)
    def _(step):
        pl.semaphore_signal(
            barrier, inc=1, device_id={"seq": (me + step) % n_seq}, device_id_type=MESH
        )

    @pl.loop(1, n_head)
    def _(step):
        pl.semaphore_signal(
            barrier, inc=1, device_id={"head": (z + step) % n_head}, device_id_type=MESH
        )

    d_copy.wait()
    lane = lax.broadcasted_iota(jnp.int32, (heads, 128), 1)
    start = None
    for n in range(chunks):
        lo = n * CHUNK
        x0 = lanes_scan(d_ref[:, lo : lo + HALF] * LOG2E, lane)
        x1 = lanes_scan(d_ref[:, lo + HALF : lo + CHUNK] * LOG2E, lane)
        x1 = x1 + jnp.broadcast_to(x0[:, 127:128], (heads, 128))
        last = jnp.broadcast_to(x1[:, 127:128], (heads, 128))
        factors = jnp.exp2(last)
        decays = jnp.exp2(last - x0), jnp.exp2(last - x1)
        if n % per_page == 0:
            start = jnp.zeros_like(last)
        begins = jnp.exp2(start)
        start = start + last
        pages = jnp.exp2(start)
        for h in range(heads):
            row = slice(h, h + 1)
            c_ref[h, :, lo : lo + HALF] = x0[row]
            c_ref[h, :, lo + HALF : lo + CHUNK] = x1[row]
            f_ref[h, :, lo : lo + HALF] = decays[0][row]
            f_ref[h, :, lo + HALF : lo + CHUNK] = decays[1][row]
            a_ref[h * chunks + n] = factors[row]
            b_ref[h * chunks + n] = begins[row]
            if n % per_page == per_page - 1:
                pd_ref[h * 2 + n // per_page] = pages[row]

    pl.semaphore_wait(barrier, n_seq - 1 + n_head - 1)

    sub = lax.broadcasted_iota(jnp.int32, (8, 128), 0)

    def send_slice(j):
        return pltpu.make_async_remote_copy(
            src_ref=sendbuf.at[j],
            dst_ref=recvbuf.at[me],
            send_sem=a_send,
            recv_sem=a_recv,
            device_id={"seq": j},
            device_id_type=MESH,
        )

    @pl.loop(0, heads)
    def _(step):
        h = (g + step) % heads
        for copy in kv_copies(step):
            copy.wait()
        ends = []
        state = None
        for n in range(chunks):
            lo = n * CHUNK
            kt = kb[h, lo : lo + CHUNK, :].T
            scaled = (kt.astype(F32) * f_ref[h, :, lo : lo + CHUNK]).astype(BF)
            update = jnp.dot(scaled, vb[h, lo : lo + CHUNK, :], preferred_element_type=F32)
            if n % per_page == 0:
                state = update
                sl[h * chunks + n] = jnp.zeros_like(update)
            else:
                sl[h * chunks + n] = state
                state = a_ref[h * chunks + n] * state + update
            if n % per_page == per_page - 1:
                ends.append(state)
        up[h] = ends[0]
        decays = jnp.concatenate(
            [
                three_parts(pd_ref[2 * h], sub),
                three_parts(pd_ref[2 * h + 1], sub),
            ],
            axis=0,
        ).astype(BF)
        for part in range(parts):
            j = h * parts + part
            first = ends[0][part * rows : (part + 1) * rows].astype(BF)
            second = ends[1][part * rows : (part + 1) * rows].astype(BF)

            @pl.when(j != me)
            def _():
                sendbuf[j, 0:rows] = first
                sendbuf[j, rows : 2 * rows] = second
                sendbuf[j, 2 * rows : 2 * rows + 16] = decays
                send_slice(j).start()

            @pl.when(j == me)
            def _():
                recvbuf[me, 0:rows] = first
                recvbuf[me, rows : 2 * rows] = second
                recvbuf[me, 2 * rows : 2 * rows + 16] = decays

    tri = lax.broadcasted_iota(jnp.int32, (HALF, HALF), 0) >= lax.broadcasted_iota(
        jnp.int32, (HALF, HALF), 1
    )

    def intra(h):
        q_copy(h).wait()
        for n in range(chunks):
            lo = n * CHUNK
            q = qb[h, lo : lo + CHUNK, :]
            k = kb[h, lo : lo + CHUNK, :]
            row0 = c_ref[h, :, lo : lo + HALF]
            row1 = c_ref[h, :, lo + HALF : lo + CHUNK]
            col0, col1 = column_of(row0), column_of(row1)
            scores = lax.dot_general(
                q, k, (((1,), (1,)), ((), ())), preferred_element_type=F32
            )
            w00 = scores[:HALF, :HALF] * jnp.exp2(jnp.where(tri, col0 - row0, -1e30))
            w10 = scores[HALF:, :HALF] * jnp.exp2(col1 - row0)
            w11 = scores[HALF:, HALF:] * jnp.exp2(jnp.where(tri, col1 - row1, -1e30))
            acc[h, lo : lo + HALF, :] = jnp.dot(
                w00.astype(BF), vb[h, lo : lo + HALF, :], preferred_element_type=F32
            )
            acc[h, lo + HALF : lo + CHUNK, :] = jnp.dot(
                jnp.concatenate([w10.astype(BF), w11.astype(BF)], axis=1),
                vb[h, lo : lo + CHUNK, :],
                preferred_element_type=F32,
            )
            qb[h, lo : lo + HALF, :] = (q[:HALF].astype(F32) * jnp.exp2(col0)).astype(BF)
            qb[h, lo + HALF : lo + CHUNK, :] = (q[HALF:].astype(F32) * jnp.exp2(col1)).astype(BF)

    pl.loop(0, INTRA_EARLY)(intra)

    pltpu.make_async_copy(
        recvbuf.at[pl.ds(0, n_seq - 1)], recvbuf.at[pl.ds(0, n_seq - 1)], a_recv
    ).wait()
    snap[0] = jnp.zeros((rows, HD), BF)

    def pages_of(i, state):
        decays = recvbuf[i, 2 * rows : 2 * rows + 16].astype(F32)
        a0 = decays[0:1] + decays[1:2] + decays[2:3]
        a1 = decays[8:9] + decays[9:10] + decays[10:11]
        state = a0 * state + recvbuf[i, 0:rows].astype(F32)
        snap[2 * i + 1] = state.astype(BF)
        state = a1 * state + recvbuf[i, rows : 2 * rows].astype(F32)
        snap[2 * i + 2] = state.astype(BF)
        return state

    lax.fori_loop(0, n_seq, pages_of, jnp.zeros((rows, HD), F32), unroll=4)

    def send_entry(i):
        return pltpu.make_async_remote_copy(
            src_ref=snap.at[2 * i],
            dst_ref=ent.at[g, pl.ds(r0, rows), :],
            send_sem=e_send,
            recv_sem=e_recv,
            device_id={"seq": i},
            device_id_type=MESH,
        )

    @pl.loop(1, n_seq)
    def _(step):
        send_entry((me + step) % n_seq).start()

    ent[g, pl.ds(r0, rows), :] = snap[2 * me]

    def send_pages(i):
        return pltpu.make_async_remote_copy(
            src_ref=pagebuf.at[pl.ds(i * SLOTS, SLOTS)],
            dst_ref=cache_hbm.at[:, g, pl.ds(r0, rows), :],
            send_sem=p_send,
            recv_sem=p_recv,
            device_id={"seq": i},
            device_id_type=MESH,
        )

    own_pages = pltpu.make_async_copy(
        pagebuf.at[pl.ds(me * SLOTS, SLOTS)], cache_hbm.at[:, g, pl.ds(r0, rows), :], p_self
    )

    def fill(i):
        for s in range(SLOTS):
            pagebuf[i * SLOTS + s] = snap[idx_ref[i * SLOTS + s]]

    @pl.loop(1, n_seq)
    def _(step):
        i = (me + step) % n_seq
        fill(i)
        send_pages(i).start()

    fill(me)
    own_pages.start()

    pl.loop(INTRA_EARLY, heads)(intra)

    pltpu.make_async_copy(
        snap.at[pl.ds(0, n_seq - 1)], snap.at[pl.ds(0, n_seq - 1)], e_recv
    ).wait()

    @pl.loop(0, heads)
    def _(h):
        en[h] = ent[h].astype(F32)
        en[heads + h] = pd_ref[2 * h] * ent[h].astype(F32) + up[h]

    def send_squares(half, step):
        return pltpu.make_async_remote_copy(
            src_ref=sq_send.at[half],
            dst_ref=sq_recv.at[half, step - 1],
            send_sem=s_send.at[half],
            recv_sem=s_recv.at[half],
            device_id={"head": (z + step) % n_head},
            device_id_type=MESH,
        )

    def finish(half):
        @pl.loop(0, per_page)
        def _(m):
            n = half * per_page + m
            lo = pl.multiple_of(n * CHUNK, CHUNK)
            squares = None
            for h in range(heads):
                state = (
                    sl[h * chunks + n] + b_ref[h * chunks + n] * en[half * heads + h]
                ).astype(BF)
                out = acc[h, pl.ds(lo, CHUNK), :] + jnp.dot(
                    qb[h, pl.ds(lo, CHUNK), :], state, preferred_element_type=F32
                )
                acc[h, pl.ds(lo, CHUNK), :] = out
                squares = out * out if squares is None else squares + out * out
            sq_send[half, 2 * m] = jnp.sum(squares[:HALF].T, axis=0, keepdims=True)
            sq_send[half, 2 * m + 1] = jnp.sum(squares[HALF:].T, axis=0, keepdims=True)

        for step in range(1, n_head):
            send_squares(half, step).start()

    def out_copy(n):
        lo = pl.multiple_of(n * CHUNK, CHUNK)
        return pltpu.make_async_copy(
            ob.at[pl.ds(lo, CHUNK), :], att_hbm.at[pl.ds(lo, CHUNK), :], o_sem
        )

    def normalize(half):
        received = sq_recv.at[half]
        pltpu.make_async_copy(received, received, s_recv.at[half]).wait()
        total = sq_send[half]
        for step in range(n_head - 1):
            total = total + sq_recv[half, step]
        scale_ref[...] = lax.rsqrt(total / (heads * HD * n_head) + 1e-6)

        @pl.loop(0, per_page)
        def _(m):
            n = half * per_page + m
            lo = pl.multiple_of(n * CHUNK, CHUNK)
            for side in range(2):
                scale = column_of(scale_ref[2 * m + side])
                at = pl.ds(pl.multiple_of(lo + side * HALF, HALF), HALF)
                for h in range(heads):
                    ob[at, h * HD : (h + 1) * HD] = (
                        acc[h, at, :] * scale * g_ref[h : h + 1, :]
                    ).astype(BF)
            out_copy(n).start()

    finish(0)
    finish(1)
    g_copy.wait()
    normalize(0)
    normalize(1)

    pltpu.make_async_copy(ob, att_hbm, o_sem).wait()
    own_pages.wait()
    sent = sendbuf.at[pl.ds(0, n_seq - 1)]
    pltpu.make_async_copy(sent, sent, a_send).wait()
    entries = snap.at[pl.ds(0, n_seq - 1)]
    pltpu.make_async_copy(entries, entries, e_send).wait()
    for half in range(2):
        received = sq_recv.at[half]
        pltpu.make_async_copy(received, received, s_send.at[half]).wait()
    pages = pagebuf.at[pl.ds(0, (n_seq - 1) * SLOTS)]
    pltpu.make_async_copy(pages, pages, p_send).wait()
    pltpu.make_async_copy(pages, pages, p_recv).wait()


def shards(n_seq, n_head, queries, key_rows, value_rows, decay_log, norm_gain, page_owner):
    toks, width = queries.shape
    heads = decay_log.shape[0]
    chunks = toks // CHUNK
    rows = HD * heads // n_seq
    n_pages = page_owner.shape[0]
    order = jnp.arange(n_pages, dtype=jnp.int32)
    earlier = (page_owner[:, None] == page_owner[None, :]) & (order[:, None] < order[None, :])
    slot = jnp.sum(earlier.astype(jnp.int32), axis=0)
    target = page_owner * SLOTS + slot
    wanted = target[None, :] == jnp.arange(n_seq * SLOTS, dtype=jnp.int32)[:, None]
    index = jnp.sum(jnp.where(wanted, order[None, :] + 1, 0), axis=1).astype(jnp.int32)
    anywhere = pl.BlockSpec(memory_space=pl.ANY)
    dma = pltpu.SemaphoreType.DMA
    return pl.pallas_call(
        functools.partial(kernel, n_seq, n_head),
        out_shape=(
            jax.ShapeDtypeStruct((toks, width), BF),
            jax.ShapeDtypeStruct((SLOTS, heads, HD, HD), BF),
        ),
        in_specs=[pl.BlockSpec(memory_space=pltpu.SMEM)] + [anywhere] * 5,
        out_specs=(anywhere, anywhere),
        scratch_shapes=[
            pltpu.VMEM((heads, toks, HD), BF),
            pltpu.VMEM((heads, toks, HD), BF),
            pltpu.VMEM((heads, toks, HD), BF),
            pltpu.VMEM((heads, toks, HD), F32),
            pltpu.VMEM((toks, width), BF),
            pltpu.VMEM((heads * chunks, HD, HD), F32),
            pltpu.VMEM((heads, HD, HD), F32),
            pltpu.VMEM((2 * heads, HD, HD), F32),
            pltpu.VMEM((heads, toks), F32),
            pltpu.VMEM((heads, HD), F32),
            pltpu.VMEM((heads, 1, toks), F32),
            pltpu.VMEM((heads, 1, toks), F32),
            pltpu.VMEM((heads * chunks, 1, 128), F32),
            pltpu.VMEM((heads * chunks, 1, 128), F32),
            pltpu.VMEM((heads * 2, 1, 128), F32),
            pltpu.VMEM((n_seq, 2 * rows + 16, HD), BF),
            pltpu.VMEM((n_seq, 2 * rows + 16, HD), BF),
            pltpu.VMEM((n_pages + 1, rows, HD), BF),
            pltpu.VMEM((n_seq * SLOTS, rows, HD), BF),
            pltpu.VMEM((heads, HD, HD), BF),
            pltpu.VMEM((2, 8, 1, 128), F32),
            pltpu.VMEM((2, n_head - 1, 8, 1, 128), F32),
            pltpu.VMEM((8, 1, 128), F32),
            dma((2, heads)),
            dma((heads,)),
            dma((2,)),
            dma,
            dma,
            dma,
            dma,
            dma,
            dma,
            dma,
            dma((2,)),
            dma((2,)),
            dma,
        ],
        compiler_params=pltpu.CompilerParams(
            collective_id=0, has_side_effects=True, vmem_limit_bytes=48 * 1024 * 1024
        ),
    )(
        index,
        queries,
        key_rows,
        value_rows,
        decay_log,
        norm_gain.reshape(heads, HD),
    )


def solution(mesh):
    return jax.shard_map(
        functools.partial(shards, mesh.shape["seq"], mesh.shape["head"]),
        mesh=mesh,
        in_specs=(
            P("seq", "head"),
            P("seq", "head"),
            P("seq", "head"),
            P("head", "seq"),
            P("head"),
            P(),
        ),
        out_specs=(P("seq", "head"), P("seq", "head", None, None)),
        check_vma=False,
    )
```

```python
import functools

import jax
import jax.numpy as jnp
from jax import lax
from jax.experimental import pallas as pl
from jax.experimental.pallas import tpu as pltpu
from jax.sharding import PartitionSpec as P

SLOTS = 5
HD = 128
HALF = 128
CHUNK = 256
LOG2E = 1.4426950408889634
BF = jnp.bfloat16
F32 = jnp.float32
MESH = pl.DeviceIdType.MESH
FIRST = 1
SECOND = 3
STAGES = 2


def lanes_scan(x, lane):
    for shift in (1, 2, 4, 8, 16, 32, 64):
        x = x + jnp.where(lane >= shift, pltpu.roll(x, shift, axis=1), 0.0)
    return x


def far_first(a):
    return 2 + a - lax.div(a, 2) * (2 * a - 1)


def column_of(row):
    return jnp.broadcast_to(row, (HALF, HALF)).T


def kernel(
    n_seq,
    n_head,
    idx_ref,
    q_hbm,
    k_hbm,
    v_hbm,
    d_hbm,
    g_hbm,
    att_hbm,
    cache_hbm,
    qb,
    kb,
    vb,
    acc,
    ec,
    ob,
    sl,
    d_ref,
    g_ref,
    c_ref,
    f_ref,
    a_ref,
    b_ref,
    b2_ref,
    pd_ref,
    dec_recv,
    sendbuf,
    recvbuf,
    snap,
    pagebuf,
    ent,
    sq_send,
    sq_recv,
    scale_ref,
    in_sem,
    q_sem,
    small_sem,
    d_send,
    d_recv,
    a_send,
    a_recv,
    e_send,
    e_recv,
    p_send,
    p_recv,
    p_self,
    s_send,
    s_recv,
    o_sem,
):
    heads, toks = kb.shape[0], kb.shape[1]
    chunks = toks // CHUNK
    per_page = chunks // 2
    classes = heads // STAGES
    parts = n_seq // classes
    rows = HD // parts
    me = lax.axis_index("seq")
    z = lax.axis_index("head")
    x, y, core = lax.div(me, 8), lax.rem(lax.div(me, 2), 4), lax.rem(me, 2)
    mine = lax.rem(x + y, classes)
    r0 = pl.multiple_of((x * 2 + core) * rows, rows)

    steps = (2, 1, 3, 0)
    at_y = [lax.rem(y + d, 4) * 2 for d in steps]
    at_core = [1 - core, core]

    def each_other(visit):
        @pl.loop(0, 4)
        def _(a):
            at_x = lax.rem(x + far_first(a), 4) * 8
            for i in range(4):
                for k in range(2):
                    j = at_x + at_y[i] + at_core[k]
                    if i == 3 and k == 1:
                        pl.when(a < 3)(functools.partial(visit, j))
                    else:
                        visit(j)

    def class_of(j):
        return lax.rem(lax.div(j, 8) + lax.rem(lax.div(j, 2), 4), classes)

    def keeper(cls, px, pc):
        return (px * 4 + lax.rem(cls + 4 - px, 4)) * 2 + pc

    def class_at(s):
        return lax.rem(mine + far_first(s), classes)

    def kv_copies(stage, s):
        h = stage * classes + class_at(s)
        hc = pl.multiple_of(h * HD, HD)
        at = stage * classes + s
        return (
            pltpu.make_async_copy(k_hbm.at[:, pl.ds(hc, HD)], kb.at[h], in_sem.at[0, at]),
            pltpu.make_async_copy(v_hbm.at[:, pl.ds(hc, HD)], vb.at[h], in_sem.at[1, at]),
        )

    def q_copy(h):
        hc = pl.multiple_of(h * HD, HD)
        return pltpu.make_async_copy(q_hbm.at[:, pl.ds(hc, HD)], qb.at[h], q_sem.at[h])

    d_copy = pltpu.make_async_copy(d_hbm, d_ref, small_sem.at[0])
    g_copy = pltpu.make_async_copy(g_hbm, g_ref, small_sem.at[1])
    d_copy.start()
    for stage in range(STAGES):

        @pl.loop(0, classes)
        def _(s):
            for copy in kv_copies(stage, s):
                copy.start()

    barrier = pltpu.get_barrier_semaphore()

    each_other(
        lambda j: pl.semaphore_signal(
            barrier, inc=1, device_id={"seq": j}, device_id_type=MESH
        )
    )
    for step in range(1, n_head):
        pl.semaphore_signal(
            barrier, inc=1, device_id={"head": lax.rem(z + step, n_head)}, device_id_type=MESH
        )

    d_copy.wait()
    lane = lax.broadcasted_iota(jnp.int32, (heads, 128), 1)
    start = whole = None
    for n in range(chunks):
        lo = n * CHUNK
        x0 = lanes_scan(d_ref[:, lo : lo + HALF] * LOG2E, lane)
        x1 = lanes_scan(d_ref[:, lo + HALF : lo + CHUNK] * LOG2E, lane)
        x1 = x1 + jnp.broadcast_to(x0[:, 127:128], (heads, 128))
        last = jnp.broadcast_to(x1[:, 127:128], (heads, 128))
        factors = jnp.exp2(last)
        decays = jnp.exp2(last - x0), jnp.exp2(last - x1)
        if n == 0:
            whole = jnp.zeros_like(last)
        if n % per_page == 0:
            start = jnp.zeros_like(last)
        begins, begins2 = jnp.exp2(start), jnp.exp2(whole)
        start, whole = start + last, whole + last
        pages = jnp.exp2(start)
        for h in range(heads):
            row = slice(h, h + 1)
            c_ref[h, :, lo : lo + HALF] = x0[row]
            c_ref[h, :, lo + HALF : lo + CHUNK] = x1[row]
            f_ref[h, :, lo : lo + HALF] = decays[0][row]
            f_ref[h, :, lo + HALF : lo + CHUNK] = decays[1][row]
            a_ref[h * chunks + n] = factors[row]
            b_ref[h * chunks + n] = begins[row]
            b2_ref[h * chunks + n] = begins2[row]
            if n % per_page == per_page - 1:
                pd_ref[h % classes, h // classes, n // per_page] = pages[row]

    def send_decays(j):
        return pltpu.make_async_remote_copy(
            src_ref=pd_ref.at[class_of(j)],
            dst_ref=dec_recv.at[me],
            send_sem=d_send,
            recv_sem=d_recv,
            device_id={"seq": j},
            device_id_type=MESH,
        )

    dec_recv[me] = pd_ref[mine]

    def send_rows(stage, j):
        return pltpu.make_async_remote_copy(
            src_ref=sendbuf.at[stage, j],
            dst_ref=recvbuf.at[stage, me],
            send_sem=a_send.at[stage],
            recv_sem=a_recv.at[stage],
            device_id={"seq": j},
            device_id_type=MESH,
        )

    def send_class(stage, cls):
        @pl.loop(0, 4)
        def _(a):
            for side in range(2):
                j = keeper(cls, lax.rem(x + far_first(a), 4), side)

                @pl.when(j != me)
                def _():
                    send_rows(stage, j).start()

                @pl.when(j == me)
                def _():
                    recvbuf[stage, me] = sendbuf[stage, me]

    def states(stage):
        @pl.loop(0, classes)
        def _(s):
            cls = class_at(s)
            h = stage * classes + cls
            for copy in kv_copies(stage, s):
                copy.wait()
            ends = []
            state = None
            for n in range(chunks):
                lo = n * CHUNK
                kt = kb[h, lo : lo + CHUNK, :].T
                scaled = (kt.astype(F32) * f_ref[h, :, lo : lo + CHUNK]).astype(BF)
                update = jnp.dot(scaled, vb[h, lo : lo + CHUNK, :], preferred_element_type=F32)
                if n == 0:
                    sl[h * chunks] = jnp.zeros_like(update, BF)
                elif n < per_page:
                    sl[h * chunks + n] = state.astype(BF)
                elif n == per_page:
                    sl[h * chunks + n] = ends[0].astype(BF)
                else:
                    sl[h * chunks + n] = (state + b_ref[h * chunks + n] * ends[0]).astype(BF)
                state = update if n % per_page == 0 else a_ref[h * chunks + n] * state + update
                if n % per_page == per_page - 1:
                    ends.append(state)
            for part in range(parts):
                j = keeper(cls, part // 2, part % 2)
                for page in range(2):
                    sendbuf[stage, j, page] = ends[page][part * rows : (part + 1) * rows].astype(BF)

            if stage > 0:
                send_class(stage, cls)

    tri = lax.broadcasted_iota(jnp.int32, (HALF, HALF), 0) >= lax.broadcasted_iota(
        jnp.int32, (HALF, HALF), 1
    )

    def intra(h):
        q_copy(h).wait()
        for n in range(chunks):
            lo = n * CHUNK
            q = qb[h, lo : lo + CHUNK, :]
            k = kb[h, lo : lo + CHUNK, :]
            row0 = c_ref[h, :, lo : lo + HALF]
            row1 = c_ref[h, :, lo + HALF : lo + CHUNK]
            col0, col1 = column_of(row0), column_of(row1)
            scores = lax.dot_general(
                q, k, (((1,), (1,)), ((), ())), preferred_element_type=F32
            )
            w00 = scores[:HALF, :HALF] * jnp.exp2(jnp.where(tri, col0 - row0, -1e30))
            w10 = scores[HALF:, :HALF] * jnp.exp2(col1 - row0)
            w11 = scores[HALF:, HALF:] * jnp.exp2(jnp.where(tri, col1 - row1, -1e30))
            out0 = jnp.dot(w00.astype(BF), vb[h, lo : lo + HALF, :], preferred_element_type=F32)
            out1 = jnp.dot(
                jnp.concatenate([w10.astype(BF), w11.astype(BF)], axis=1),
                vb[h, lo : lo + CHUNK, :],
                preferred_element_type=F32,
            )
            e0, e1 = jnp.exp2(col0), jnp.exp2(col1)
            if n > 0:
                carried = jnp.dot(q, sl[h * chunks + n], preferred_element_type=F32)
                out0 = out0 + e0 * carried[:HALF]
                out1 = out1 + e1 * carried[HALF:]
            acc[h, lo : lo + HALF, :] = out0
            acc[h, lo + HALF : lo + CHUNK, :] = out1
            ec[h, lo : lo + HALF, :] = e0
            ec[h, lo + HALF : lo + CHUNK, :] = e1

    def wait_rows(stage):
        arrived = recvbuf.at[stage, pl.ds(0, n_seq - 1)]
        pltpu.make_async_copy(arrived, arrived, a_recv.at[stage]).wait()

    def recur(stage):
        snap[0, stage] = jnp.zeros((rows, HD), BF)

        def pages_of(i, state):
            state = dec_recv[i, stage, 0] * state + recvbuf[stage, i, 0].astype(F32)
            snap[2 * i + 1, stage] = state.astype(BF)
            state = dec_recv[i, stage, 1] * state + recvbuf[stage, i, 1].astype(F32)
            snap[2 * i + 2, stage] = state.astype(BF)
            return state

        lax.fori_loop(0, n_seq, pages_of, jnp.zeros((rows, HD), F32), unroll=8)

    def send_entry(i):
        return pltpu.make_async_remote_copy(
            src_ref=snap.at[2 * i],
            dst_ref=ent.at[:, mine, pl.ds(r0, rows), :],
            send_sem=e_send,
            recv_sem=e_recv,
            device_id={"seq": i},
            device_id_type=MESH,
        )

    def kept(stage):
        return cache_hbm.at[:, stage * classes + mine, pl.ds(r0, rows), :]

    def send_pages(stage, i):
        return pltpu.make_async_remote_copy(
            src_ref=pagebuf.at[stage, pl.ds(i * SLOTS, SLOTS)],
            dst_ref=kept(stage),
            send_sem=p_send.at[stage],
            recv_sem=p_recv.at[stage],
            device_id={"seq": i},
            device_id_type=MESH,
        )

    def own_pages(stage):
        return pltpu.make_async_copy(
            pagebuf.at[stage, pl.ds(me * SLOTS, SLOTS)], kept(stage), p_self.at[stage]
        )

    def hand_out(stage):
        def fill(i):
            for s in range(SLOTS):
                pagebuf[stage, i * SLOTS + s] = snap[idx_ref[i * SLOTS + s], stage]

        def visit(i):
            fill(i)
            send_pages(stage, i).start()

        each_other(visit)
        fill(me)
        own_pages(stage).start()

    states(0)
    pl.semaphore_wait(barrier, n_seq - 1 + n_head - 1)
    each_other(lambda j: send_decays(j).start())
    each_other(lambda j: send_rows(0, j).start())
    recvbuf[0, me] = sendbuf[0, me]

    @pl.loop(0, heads)
    def _(h):
        q_copy(h).start()

    g_copy.start()
    states(1)
    pl.loop(0, FIRST)(intra)
    all_decays = dec_recv.at[pl.ds(0, n_seq - 1)]
    pltpu.make_async_copy(all_decays, all_decays, d_recv).wait()
    wait_rows(0)
    recur(0)
    hand_out(0)
    pl.loop(FIRST, SECOND)(intra)
    wait_rows(1)
    recur(1)
    each_other(lambda i: send_entry(i).start())
    ent[:, mine, pl.ds(r0, rows), :] = snap[2 * me]

    hand_out(1)
    pl.loop(SECOND, heads)(intra)

    entries = snap.at[pl.ds(0, n_seq - 1)]
    pltpu.make_async_copy(entries, entries, e_recv).wait()

    def send_squares(half, step):
        return pltpu.make_async_remote_copy(
            src_ref=sq_send.at[half],
            dst_ref=sq_recv.at[half, step - 1],
            send_sem=s_send.at[half],
            recv_sem=s_recv.at[half],
            device_id={"head": lax.rem(z + step, n_head)},
            device_id_type=MESH,
        )

    def finish(half):
        @pl.loop(0, per_page)
        def _(m):
            n = half * per_page + m
            lo = pl.multiple_of(n * CHUNK, CHUNK)
            squares = None
            for h in range(heads):
                carried = jnp.dot(
                    qb[h, pl.ds(lo, CHUNK), :],
                    ent[h // classes, h % classes],
                    preferred_element_type=F32,
                )
                scale = ec[h, pl.ds(lo, CHUNK), :] * b2_ref[h * chunks + n]
                out = acc[h, pl.ds(lo, CHUNK), :] + scale * carried
                acc[h, pl.ds(lo, CHUNK), :] = out
                squares = out * out if squares is None else squares + out * out
            sq_send[half, 2 * m] = jnp.sum(squares[:HALF].T, axis=0, keepdims=True)
            sq_send[half, 2 * m + 1] = jnp.sum(squares[HALF:].T, axis=0, keepdims=True)

        for step in range(1, n_head):
            send_squares(half, step).start()

    def out_copy(n):
        lo = pl.multiple_of(n * CHUNK, CHUNK)
        return pltpu.make_async_copy(
            ob.at[pl.ds(lo, CHUNK), :], att_hbm.at[pl.ds(lo, CHUNK), :], o_sem
        )

    def normalize(half):
        received = sq_recv.at[half]
        pltpu.make_async_copy(received, received, s_recv.at[half]).wait()
        total = sq_send[half]
        for step in range(n_head - 1):
            total = total + sq_recv[half, step]
        scale_ref[...] = lax.rsqrt(total / (heads * HD * n_head) + 1e-6)

        @pl.loop(0, per_page)
        def _(m):
            n = half * per_page + m
            lo = pl.multiple_of(n * CHUNK, CHUNK)
            for side in range(2):
                scale = column_of(scale_ref[2 * m + side])
                at = pl.ds(pl.multiple_of(lo + side * HALF, HALF), HALF)
                for h in range(heads):
                    ob[at, h * HD : (h + 1) * HD] = (
                        acc[h, at, :] * scale * g_ref[h : h + 1, :]
                    ).astype(BF)
            out_copy(n).start()

    finish(0)
    finish(1)
    g_copy.wait()
    normalize(0)
    normalize(1)

    pltpu.make_async_copy(entries, entries, e_send).wait()
    pltpu.make_async_copy(ob, att_hbm, o_sem).wait()
    pltpu.make_async_copy(all_decays, all_decays, d_send).wait()
    for half in range(2):
        received = sq_recv.at[half]
        pltpu.make_async_copy(received, received, s_send.at[half]).wait()
    for stage in range(STAGES):
        sent = sendbuf.at[stage, pl.ds(0, n_seq - 1)]
        pltpu.make_async_copy(sent, sent, a_send.at[stage]).wait()
        own_pages(stage).wait()
        pages = pagebuf.at[stage, pl.ds(0, (n_seq - 1) * SLOTS)]
        pltpu.make_async_copy(pages, pages, p_send.at[stage]).wait()
        pltpu.make_async_copy(pages, pages, p_recv.at[stage]).wait()


def shards(n_seq, n_head, queries, key_rows, value_rows, decay_log, norm_gain, page_owner):
    toks, width = queries.shape
    heads = decay_log.shape[0]
    chunks = toks // CHUNK
    classes = heads // STAGES
    rows = HD * classes // n_seq
    n_pages = page_owner.shape[0]
    order = jnp.arange(n_pages, dtype=jnp.int32)
    earlier = (page_owner[:, None] == page_owner[None, :]) & (order[:, None] < order[None, :])
    slot = jnp.sum(earlier.astype(jnp.int32), axis=0)
    target = page_owner * SLOTS + slot
    wanted = target[None, :] == jnp.arange(n_seq * SLOTS, dtype=jnp.int32)[:, None]
    index = jnp.sum(jnp.where(wanted, order[None, :] + 1, 0), axis=1).astype(jnp.int32)
    anywhere = pl.BlockSpec(memory_space=pl.ANY)
    dma = pltpu.SemaphoreType.DMA
    return pl.pallas_call(
        functools.partial(kernel, n_seq, n_head),
        out_shape=(
            jax.ShapeDtypeStruct((toks, width), BF),
            jax.ShapeDtypeStruct((SLOTS, heads, HD, HD), BF),
        ),
        in_specs=[pl.BlockSpec(memory_space=pltpu.SMEM)]
        + [pl.BlockSpec(memory_space=pltpu.HBM)] * 5,
        out_specs=(anywhere, anywhere),
        scratch_shapes=[
            pltpu.VMEM((heads, toks, HD), BF),
            pltpu.VMEM((heads, toks, HD), BF),
            pltpu.VMEM((heads, toks, HD), BF),
            pltpu.VMEM((heads, toks, HD), F32),
            pltpu.VMEM((heads, toks, HD), F32),
            pltpu.VMEM((toks, width), BF),
            pltpu.VMEM((heads * chunks, HD, HD), BF),
            pltpu.VMEM((heads, toks), F32),
            pltpu.VMEM((heads, HD), F32),
            pltpu.VMEM((heads, 1, toks), F32),
            pltpu.VMEM((heads, 1, toks), F32),
            pltpu.VMEM((heads * chunks, 1, 128), F32),
            pltpu.VMEM((heads * chunks, 1, 128), F32),
            pltpu.VMEM((heads * chunks, 1, 128), F32),
            pltpu.VMEM((classes, STAGES, 2, 1, 128), F32),
            pltpu.VMEM((n_seq, STAGES, 2, 1, 128), F32),
            pltpu.VMEM((STAGES, n_seq, 2, rows, HD), BF),
            pltpu.VMEM((STAGES, n_seq, 2, rows, HD), BF),
            pltpu.VMEM((n_pages + 1, STAGES, rows, HD), BF),
            pltpu.VMEM((STAGES, n_seq * SLOTS, rows, HD), BF),
            pltpu.VMEM((STAGES, classes, HD, HD), BF),
            pltpu.VMEM((2, 8, 1, 128), F32),
            pltpu.VMEM((2, n_head - 1, 8, 1, 128), F32),
            pltpu.VMEM((8, 1, 128), F32),
            dma((2, heads)),
            dma((heads,)),
            dma((2,)),
            dma,
            dma,
            dma((STAGES,)),
            dma((STAGES,)),
            dma,
            dma,
            dma((STAGES,)),
            dma((STAGES,)),
            dma((STAGES,)),
            dma((2,)),
            dma((2,)),
            dma,
        ],
        compiler_params=pltpu.CompilerParams(
            collective_id=0, has_side_effects=True, vmem_limit_bytes=48 * 1024 * 1024
        ),
    )(
        index,
        queries,
        key_rows,
        value_rows,
        pltpu.with_memory_space_constraint(decay_log, pltpu.HBM),
        pltpu.with_memory_space_constraint(norm_gain.reshape(heads, HD), pltpu.HBM),
    )


def solution(mesh):
    return jax.shard_map(
        functools.partial(shards, mesh.shape["seq"], mesh.shape["head"]),
        mesh=mesh,
        in_specs=(
            P("seq", "head"),
            P("seq", "head"),
            P("seq", "head"),
            P("head", "seq"),
            P("head"),
            P(),
        ),
        out_specs=(P("seq", "head"), P("seq", "head", None, None)),
        check_vma=False,
    )
```

```python
import functools

import jax
import jax.numpy as jnp
from jax import lax
from jax.experimental import pallas as pl
from jax.experimental.pallas import tpu as pltpu
from jax.sharding import PartitionSpec as P

SLOTS = 5
HD = 128
HALF = 128
CHUNK = 256
LOG2E = 1.4426950408889634
BF = jnp.bfloat16
F32 = jnp.float32
MESH = pl.DeviceIdType.MESH
FIRST = 1
SECOND = 3
STAGES = 2


def lanes_scan(x, lane):
    for shift in (1, 2, 4, 8, 16, 32, 64):
        x = x + jnp.where(lane >= shift, pltpu.roll(x, shift, axis=1), 0.0)
    return x


def far_first(a):
    return 2 + a - lax.div(a, 2) * (2 * a - 1)


def column_of(row):
    return jnp.broadcast_to(row, (HALF, HALF)).T


def kernel(
    n_seq,
    n_head,
    q_hbm,
    k_hbm,
    v_hbm,
    d_hbm,
    g_hbm,
    owner_hbm,
    att_hbm,
    cache_hbm,
    qb,
    kb,
    vb,
    acc,
    ec,
    ob,
    sl,
    d_ref,
    g_ref,
    owner_ref,
    idx_vec,
    idx_ref,
    c_ref,
    f_ref,
    a_ref,
    b_ref,
    b2_ref,
    pd_ref,
    dec_recv,
    sendbuf,
    recvbuf,
    snap,
    pagebuf,
    ent,
    sq_send,
    sq_recv,
    scale_ref,
    in_sem,
    q_sem,
    small_sem,
    d_send,
    d_recv,
    a_send,
    a_recv,
    e_send,
    e_recv,
    p_send,
    p_recv,
    p_self,
    s_send,
    s_recv,
    o_sem,
):
    heads, toks = kb.shape[0], kb.shape[1]
    chunks = toks // CHUNK
    per_page = chunks // 2
    classes = heads // STAGES
    parts = n_seq // classes
    rows = HD // parts
    me = lax.axis_index("seq")
    z = lax.axis_index("head")
    x, y, core = lax.div(me, 8), lax.rem(lax.div(me, 2), 4), lax.rem(me, 2)
    mine = lax.rem(x + y, classes)
    r0 = pl.multiple_of((x * 2 + core) * rows, rows)

    steps = (2, 1, 3, 0)
    at_y = [lax.rem(y + d, 4) * 2 for d in steps]
    at_core = [1 - core, core]

    def each_other(visit):
        @pl.loop(0, 4)
        def _(a):
            at_x = lax.rem(x + far_first(a), 4) * 8
            for i in range(4):
                for k in range(2):
                    j = at_x + at_y[i] + at_core[k]
                    if i == 3 and k == 1:
                        pl.when(a < 3)(functools.partial(visit, j))
                    else:
                        visit(j)

    def class_of(j):
        return lax.rem(lax.div(j, 8) + lax.rem(lax.div(j, 2), 4), classes)

    def keeper(cls, px, pc):
        return (px * 4 + lax.rem(cls + 4 - px, 4)) * 2 + pc

    def class_at(s):
        return lax.rem(mine + far_first(s), classes)

    def kv_copies(stage, s):
        h = stage * classes + class_at(s)
        hc = pl.multiple_of(h * HD, HD)
        at = stage * classes + s
        return (
            pltpu.make_async_copy(k_hbm.at[:, pl.ds(hc, HD)], kb.at[h], in_sem.at[0, at]),
            pltpu.make_async_copy(v_hbm.at[:, pl.ds(hc, HD)], vb.at[h], in_sem.at[1, at]),
        )

    def q_copy(h):
        hc = pl.multiple_of(h * HD, HD)
        return pltpu.make_async_copy(q_hbm.at[:, pl.ds(hc, HD)], qb.at[h], q_sem.at[h])

    d_copy = pltpu.make_async_copy(d_hbm, d_ref, small_sem.at[0])
    g_copy = pltpu.make_async_copy(g_hbm, g_ref, small_sem.at[1])
    owner_copy = pltpu.make_async_copy(owner_hbm, owner_ref, small_sem.at[2])
    idx_copy = pltpu.make_async_copy(idx_vec, idx_ref, small_sem.at[3])
    d_copy.start()
    owner_copy.start()

    def load(stage):
        @pl.loop(0, classes)
        def _(s):
            for copy in kv_copies(stage, s):
                copy.start()

    load(0)
    load(1)

    barrier = pltpu.get_barrier_semaphore()

    each_other(
        lambda j: pl.semaphore_signal(
            barrier, inc=1, device_id={"seq": j}, device_id_type=MESH
        )
    )
    for step in range(1, n_head):
        pl.semaphore_signal(
            barrier, inc=1, device_id={"head": lax.rem(z + step, n_head)}, device_id_type=MESH
        )

    d_copy.wait()
    lane = lax.broadcasted_iota(jnp.int32, (heads, 128), 1)
    start = whole = None
    for n in range(chunks):
        lo = n * CHUNK
        x0 = lanes_scan(d_ref[:, lo : lo + HALF] * LOG2E, lane)
        x1 = lanes_scan(d_ref[:, lo + HALF : lo + CHUNK] * LOG2E, lane)
        x1 = x1 + jnp.broadcast_to(x0[:, 127:128], (heads, 128))
        last = jnp.broadcast_to(x1[:, 127:128], (heads, 128))
        factors = jnp.exp2(last)
        decays = jnp.exp2(last - x0), jnp.exp2(last - x1)
        if n == 0:
            whole = jnp.zeros_like(last)
        if n % per_page == 0:
            start = jnp.zeros_like(last)
        begins, begins2 = jnp.exp2(start), jnp.exp2(whole)
        start, whole = start + last, whole + last
        pages = jnp.exp2(start)
        for h in range(heads):
            row = slice(h, h + 1)
            c_ref[h, :, lo : lo + HALF] = x0[row]
            c_ref[h, :, lo + HALF : lo + CHUNK] = x1[row]
            f_ref[h, :, lo : lo + HALF] = decays[0][row]
            f_ref[h, :, lo + HALF : lo + CHUNK] = decays[1][row]
            a_ref[h * chunks + n] = factors[row]
            b_ref[h * chunks + n] = begins[row]
            b2_ref[h * chunks + n] = begins2[row]
            if n % per_page == per_page - 1:
                pd_ref[h % classes, h // classes, n // per_page] = pages[row]

    def send_decays(j):
        return pltpu.make_async_remote_copy(
            src_ref=pd_ref.at[class_of(j)],
            dst_ref=dec_recv.at[me],
            send_sem=d_send,
            recv_sem=d_recv,
            device_id={"seq": j},
            device_id_type=MESH,
        )

    dec_recv[me] = pd_ref[mine]

    def send_rows(stage, j):
        return pltpu.make_async_remote_copy(
            src_ref=sendbuf.at[stage, j],
            dst_ref=recvbuf.at[stage, me],
            send_sem=a_send.at[stage],
            recv_sem=a_recv.at[stage],
            device_id={"seq": j},
            device_id_type=MESH,
        )

    def send_class(stage, cls):
        @pl.loop(0, 4)
        def _(a):
            for side in range(2):
                j = keeper(cls, lax.rem(x + far_first(a), 4), side)

                @pl.when(j != me)
                def _():
                    send_rows(stage, j).start()

                @pl.when(j == me)
                def _():
                    recvbuf[stage, me] = sendbuf[stage, me]

    def states(stage):
        @pl.loop(0, classes)
        def _(s):
            cls = class_at(s)
            h = stage * classes + cls
            for copy in kv_copies(stage, s):
                copy.wait()
            ends = []
            state = None
            for n in range(chunks):
                lo = n * CHUNK
                kt = kb[h, lo : lo + CHUNK, :].T
                scaled = (kt.astype(F32) * f_ref[h, :, lo : lo + CHUNK]).astype(BF)
                update = jnp.dot(scaled, vb[h, lo : lo + CHUNK, :], preferred_element_type=F32)
                if n == 0:
                    sl[h * chunks] = jnp.zeros_like(update, BF)
                elif n < per_page:
                    sl[h * chunks + n] = state.astype(BF)
                elif n == per_page:
                    sl[h * chunks + n] = ends[0].astype(BF)
                else:
                    sl[h * chunks + n] = (state + b_ref[h * chunks + n] * ends[0]).astype(BF)
                state = update if n % per_page == 0 else a_ref[h * chunks + n] * state + update
                if n % per_page == per_page - 1:
                    ends.append(state)
            for part in range(parts):
                j = keeper(cls, part // 2, part % 2)
                for page in range(2):
                    sendbuf[stage, j, page] = ends[page][part * rows : (part + 1) * rows].astype(BF)

            if stage > 0:
                send_class(stage, cls)

    tri = lax.broadcasted_iota(jnp.int32, (HALF, HALF), 0) >= lax.broadcasted_iota(
        jnp.int32, (HALF, HALF), 1
    )

    def intra(h):
        q_copy(h).wait()
        for n in range(chunks):
            lo = n * CHUNK
            q = qb[h, lo : lo + CHUNK, :]
            k = kb[h, lo : lo + CHUNK, :]
            row0 = c_ref[h, :, lo : lo + HALF]
            row1 = c_ref[h, :, lo + HALF : lo + CHUNK]
            col0, col1 = column_of(row0), column_of(row1)
            scores = lax.dot_general(
                q, k, (((1,), (1,)), ((), ())), preferred_element_type=F32
            )
            w00 = scores[:HALF, :HALF] * jnp.exp2(jnp.where(tri, col0 - row0, -1e30))
            w10 = scores[HALF:, :HALF] * jnp.exp2(col1 - row0)
            w11 = scores[HALF:, HALF:] * jnp.exp2(jnp.where(tri, col1 - row1, -1e30))
            out0 = jnp.dot(w00.astype(BF), vb[h, lo : lo + HALF, :], preferred_element_type=F32)
            out1 = jnp.dot(
                jnp.concatenate([w10.astype(BF), w11.astype(BF)], axis=1),
                vb[h, lo : lo + CHUNK, :],
                preferred_element_type=F32,
            )
            e0, e1 = jnp.exp2(col0), jnp.exp2(col1)
            if n > 0:
                carried = jnp.dot(q, sl[h * chunks + n], preferred_element_type=F32)
                out0 = out0 + e0 * carried[:HALF]
                out1 = out1 + e1 * carried[HALF:]
            acc[h, lo : lo + HALF, :] = out0
            acc[h, lo + HALF : lo + CHUNK, :] = out1
            ec[h, lo : lo + HALF, :] = e0
            ec[h, lo + HALF : lo + CHUNK, :] = e1

    def wait_rows(stage):
        arrived = recvbuf.at[stage, pl.ds(0, n_seq - 1)]
        pltpu.make_async_copy(arrived, arrived, a_recv.at[stage]).wait()

    def recur(stage):
        snap[0, stage] = jnp.zeros((rows, HD), BF)

        def pages_of(i, state):
            state = dec_recv[i, stage, 0] * state + recvbuf[stage, i, 0].astype(F32)
            snap[2 * i + 1, stage] = state.astype(BF)
            state = dec_recv[i, stage, 1] * state + recvbuf[stage, i, 1].astype(F32)
            snap[2 * i + 2, stage] = state.astype(BF)
            return state

        lax.fori_loop(0, n_seq, pages_of, jnp.zeros((rows, HD), F32), unroll=8)

    def send_entry(i):
        return pltpu.make_async_remote_copy(
            src_ref=snap.at[2 * i],
            dst_ref=ent.at[:, mine, pl.ds(r0, rows), :],
            send_sem=e_send,
            recv_sem=e_recv,
            device_id={"seq": i},
            device_id_type=MESH,
        )

    def kept(stage):
        return cache_hbm.at[:, stage * classes + mine, pl.ds(r0, rows), :]

    def send_pages(stage, i):
        return pltpu.make_async_remote_copy(
            src_ref=pagebuf.at[stage, pl.ds(i * SLOTS, SLOTS)],
            dst_ref=kept(stage),
            send_sem=p_send.at[stage],
            recv_sem=p_recv.at[stage],
            device_id={"seq": i},
            device_id_type=MESH,
        )

    def own_pages(stage):
        return pltpu.make_async_copy(
            pagebuf.at[stage, pl.ds(me * SLOTS, SLOTS)], kept(stage), p_self.at[stage]
        )

    def hand_out(stage):
        def fill(i):
            for s in range(SLOTS):
                pagebuf[stage, i * SLOTS + s] = snap[idx_ref[0, i * SLOTS + s], stage]

        def visit(i):
            fill(i)
            send_pages(stage, i).start()

        each_other(visit)
        fill(me)
        own_pages(stage).start()

    owner_copy.wait()
    n_pages = owner_ref.shape[1]
    square = (n_pages, n_pages)
    above = lax.broadcasted_iota(jnp.int32, square, 0)
    across = lax.broadcasted_iota(jnp.int32, square, 1)

    def turned(row):
        spread = jnp.broadcast_to(row, square)
        return jnp.max(jnp.where(above == across, spread, 0), axis=1, keepdims=True)

    owner = owner_ref[...]
    same = (turned(owner) == owner) & (above < across)
    slot = jnp.sum(jnp.where(same, 1, 0), axis=0, keepdims=True)
    target = turned(owner * SLOTS + slot)
    wide = (n_pages, 256)
    page = lax.broadcasted_iota(jnp.int32, wide, 0)
    place = lax.broadcasted_iota(jnp.int32, wide, 1)
    found = jnp.where(target == place, page + 1, 0)
    idx_vec[...] = jnp.max(found, axis=0, keepdims=True)
    idx_copy.start()

    states(0)
    pl.semaphore_wait(barrier, n_seq - 1 + n_head - 1)
    each_other(lambda j: send_decays(j).start())
    each_other(lambda j: send_rows(0, j).start())
    recvbuf[0, me] = sendbuf[0, me]

    @pl.loop(0, heads)
    def _(h):
        q_copy(h).start()

    g_copy.start()
    states(1)
    pl.loop(0, FIRST)(intra)
    all_decays = dec_recv.at[pl.ds(0, n_seq - 1)]
    pltpu.make_async_copy(all_decays, all_decays, d_recv).wait()
    idx_copy.wait()
    wait_rows(0)
    recur(0)
    hand_out(0)
    pl.loop(FIRST, SECOND)(intra)
    wait_rows(1)
    recur(1)
    each_other(lambda i: send_entry(i).start())
    ent[:, mine, pl.ds(r0, rows), :] = snap[2 * me]

    hand_out(1)
    pl.loop(SECOND, heads)(intra)

    entries = snap.at[pl.ds(0, n_seq - 1)]
    pltpu.make_async_copy(entries, entries, e_recv).wait()

    def send_squares(half, step):
        return pltpu.make_async_remote_copy(
            src_ref=sq_send.at[half],
            dst_ref=sq_recv.at[half, step - 1],
            send_sem=s_send.at[half],
            recv_sem=s_recv.at[half],
            device_id={"head": lax.rem(z + step, n_head)},
            device_id_type=MESH,
        )

    def finish(half):
        @pl.loop(0, per_page)
        def _(m):
            n = half * per_page + m
            lo = pl.multiple_of(n * CHUNK, CHUNK)
            squares = None
            for h in range(heads):
                carried = jnp.dot(
                    qb[h, pl.ds(lo, CHUNK), :],
                    ent[h // classes, h % classes],
                    preferred_element_type=F32,
                )
                scale = ec[h, pl.ds(lo, CHUNK), :] * b2_ref[h * chunks + n]
                out = acc[h, pl.ds(lo, CHUNK), :] + scale * carried
                acc[h, pl.ds(lo, CHUNK), :] = out
                squares = out * out if squares is None else squares + out * out
            sq_send[half, 2 * m] = jnp.sum(squares[:HALF].T, axis=0, keepdims=True)
            sq_send[half, 2 * m + 1] = jnp.sum(squares[HALF:].T, axis=0, keepdims=True)

        for step in range(1, n_head):
            send_squares(half, step).start()

    def out_copy(n):
        lo = pl.multiple_of(n * CHUNK, CHUNK)
        return pltpu.make_async_copy(
            ob.at[pl.ds(lo, CHUNK), :], att_hbm.at[pl.ds(lo, CHUNK), :], o_sem
        )

    def normalize(half):
        received = sq_recv.at[half]
        pltpu.make_async_copy(received, received, s_recv.at[half]).wait()
        total = sq_send[half]
        for step in range(n_head - 1):
            total = total + sq_recv[half, step]
        scale_ref[...] = lax.rsqrt(total / (heads * HD * n_head) + 1e-6)

        @pl.loop(0, per_page)
        def _(m):
            n = half * per_page + m
            lo = pl.multiple_of(n * CHUNK, CHUNK)
            for side in range(2):
                scale = column_of(scale_ref[2 * m + side])
                at = pl.ds(pl.multiple_of(lo + side * HALF, HALF), HALF)
                for h in range(heads):
                    ob[at, h * HD : (h + 1) * HD] = (
                        acc[h, at, :] * scale * g_ref[h : h + 1, :]
                    ).astype(BF)
            out_copy(n).start()

    finish(0)
    finish(1)
    g_copy.wait()
    normalize(0)
    normalize(1)

    pltpu.make_async_copy(entries, entries, e_send).wait()
    pltpu.make_async_copy(ob, att_hbm, o_sem).wait()
    pltpu.make_async_copy(all_decays, all_decays, d_send).wait()
    for half in range(2):
        received = sq_recv.at[half]
        pltpu.make_async_copy(received, received, s_send.at[half]).wait()
    for stage in range(STAGES):
        sent = sendbuf.at[stage, pl.ds(0, n_seq - 1)]
        pltpu.make_async_copy(sent, sent, a_send.at[stage]).wait()
        own_pages(stage).wait()
        pages = pagebuf.at[stage, pl.ds(0, (n_seq - 1) * SLOTS)]
        pltpu.make_async_copy(pages, pages, p_send.at[stage]).wait()
        pltpu.make_async_copy(pages, pages, p_recv.at[stage]).wait()


def shards(n_seq, n_head, queries, key_rows, value_rows, decay_log, norm_gain, page_owner):
    toks, width = queries.shape
    heads = decay_log.shape[0]
    chunks = toks // CHUNK
    classes = heads // STAGES
    rows = HD * classes // n_seq
    n_pages = page_owner.shape[0]
    anywhere = pl.BlockSpec(memory_space=pl.ANY)
    dma = pltpu.SemaphoreType.DMA
    return pl.pallas_call(
        functools.partial(kernel, n_seq, n_head),
        out_shape=(
            jax.ShapeDtypeStruct((toks, width), BF),
            jax.ShapeDtypeStruct((SLOTS, heads, HD, HD), BF),
        ),
        in_specs=[pl.BlockSpec(memory_space=pltpu.HBM)] * 6,
        out_specs=(anywhere, anywhere),
        scratch_shapes=[
            pltpu.VMEM((heads, toks, HD), BF),
            pltpu.VMEM((heads, toks, HD), BF),
            pltpu.VMEM((heads, toks, HD), BF),
            pltpu.VMEM((heads, toks, HD), F32),
            pltpu.VMEM((heads, toks, HD), F32),
            pltpu.VMEM((toks, width), BF),
            pltpu.VMEM((heads * chunks, HD, HD), BF),
            pltpu.VMEM((heads, toks), F32),
            pltpu.VMEM((heads, HD), F32),
            pltpu.VMEM((1, n_pages), jnp.int32),
            pltpu.VMEM((1, 256), jnp.int32),
            pltpu.SMEM((1, 256), jnp.int32),
            pltpu.VMEM((heads, 1, toks), F32),
            pltpu.VMEM((heads, 1, toks), F32),
            pltpu.VMEM((heads * chunks, 1, 128), F32),
            pltpu.VMEM((heads * chunks, 1, 128), F32),
            pltpu.VMEM((heads * chunks, 1, 128), F32),
            pltpu.VMEM((classes, STAGES, 2, 1, 128), F32),
            pltpu.VMEM((n_seq, STAGES, 2, 1, 128), F32),
            pltpu.VMEM((STAGES, n_seq, 2, rows, HD), BF),
            pltpu.VMEM((STAGES, n_seq, 2, rows, HD), BF),
            pltpu.VMEM((n_pages + 1, STAGES, rows, HD), BF),
            pltpu.VMEM((STAGES, n_seq * SLOTS, rows, HD), BF),
            pltpu.VMEM((STAGES, classes, HD, HD), BF),
            pltpu.VMEM((2, 8, 1, 128), F32),
            pltpu.VMEM((2, n_head - 1, 8, 1, 128), F32),
            pltpu.VMEM((8, 1, 128), F32),
            dma((2, heads)),
            dma((heads,)),
            dma((4,)),
            dma,
            dma,
            dma((STAGES,)),
            dma((STAGES,)),
            dma,
            dma,
            dma((STAGES,)),
            dma((STAGES,)),
            dma((STAGES,)),
            dma((2,)),
            dma((2,)),
            dma,
        ],
        compiler_params=pltpu.CompilerParams(
            collective_id=0, has_side_effects=True, vmem_limit_bytes=48 * 1024 * 1024
        ),
    )(
        queries,
        key_rows,
        value_rows,
        pltpu.with_memory_space_constraint(decay_log, pltpu.HBM),
        pltpu.with_memory_space_constraint(norm_gain.reshape(heads, HD), pltpu.HBM),
        pltpu.with_memory_space_constraint(page_owner.reshape(1, n_pages), pltpu.HBM),
    )


def solution(mesh):
    return jax.shard_map(
        functools.partial(shards, mesh.shape["seq"], mesh.shape["head"]),
        mesh=mesh,
        in_specs=(
            P("seq", "head"),
            P("seq", "head"),
            P("seq", "head"),
            P("head", "seq"),
            P("head"),
            P(),
        ),
        out_specs=(P("seq", "head"), P("seq", "head", None, None)),
        check_vma=False,
    )
```

```python
import functools

import jax
import jax.numpy as jnp
from jax import lax
from jax.experimental import pallas as pl
from jax.experimental.pallas import tpu as pltpu
from jax.sharding import PartitionSpec as P

SLOTS = 5
HD = 128
HALF = 128
CHUNK = 256
LOG2E = 1.4426950408889634
BF = jnp.bfloat16
F32 = jnp.float32
MESH = pl.DeviceIdType.MESH
FIRST = 1
SECOND = 3
STAGES = 2


def lanes_scan(x, lane):
    for shift in (1, 2, 4, 8, 16, 32, 64):
        x = x + jnp.where(lane >= shift, pltpu.roll(x, shift, axis=1), 0.0)
    return x


def far_first(a):
    return 2 + a - lax.div(a, 2) * (2 * a - 1)


def column_of(row):
    return jnp.broadcast_to(row, (HALF, HALF)).T


def kernel(
    n_seq,
    n_head,
    q_hbm,
    k_hbm,
    v_hbm,
    d_hbm,
    g_hbm,
    owner_hbm,
    att_hbm,
    cache_hbm,
    qb,
    kb,
    vb,
    acc,
    ec,
    ob,
    sl,
    d_ref,
    g_ref,
    owner_ref,
    idx_vec,
    idx_ref,
    c_ref,
    f_ref,
    a_ref,
    b_ref,
    b2_ref,
    pd_ref,
    dec_recv,
    sendbuf,
    recvbuf,
    snap,
    pagebuf,
    ent,
    sq_send,
    sq_recv,
    scale_ref,
    in_sem,
    q_sem,
    small_sem,
    d_send,
    d_recv,
    a_send,
    a_recv,
    e_send,
    e_recv,
    p_send,
    p_recv,
    p_self,
    s_send,
    s_recv,
    o_sem,
):
    heads, toks = kb.shape[0], kb.shape[1]
    chunks = toks // CHUNK
    per_page = chunks // 2
    classes = heads // STAGES
    parts = n_seq // classes
    rows = HD // parts
    me = lax.axis_index("seq")
    z = lax.axis_index("head")
    x, y, core = lax.div(me, 8), lax.rem(lax.div(me, 2), 4), lax.rem(me, 2)
    mine = lax.rem(x + y, classes)
    r0 = pl.multiple_of((x * 2 + core) * rows, rows)

    steps = (2, 1, 3, 0)
    at_y = [lax.rem(y + d, 4) * 2 for d in steps]
    at_core = [1 - core, core]

    def each_other(visit):
        @pl.loop(0, 4)
        def _(a):
            at_x = lax.rem(x + far_first(a), 4) * 8
            for i in range(4):
                for k in range(2):
                    j = at_x + at_y[i] + at_core[k]
                    if i == 3 and k == 1:
                        pl.when(a < 3)(functools.partial(visit, j))
                    else:
                        visit(j)

    def class_of(j):
        return lax.rem(lax.div(j, 8) + lax.rem(lax.div(j, 2), 4), classes)

    def keeper(cls, px, pc):
        return (px * 4 + lax.rem(cls + 4 - px, 4)) * 2 + pc

    def class_at(s):
        return lax.rem(mine + far_first(s), classes)

    def kv_copies(stage, s):
        h = stage * classes + class_at(s)
        hc = pl.multiple_of(h * HD, HD)
        at = stage * classes + s
        return (
            pltpu.make_async_copy(k_hbm.at[:, pl.ds(hc, HD)], kb.at[h], in_sem.at[0, at]),
            pltpu.make_async_copy(v_hbm.at[:, pl.ds(hc, HD)], vb.at[h], in_sem.at[1, at]),
        )

    def q_copy(h):
        hc = pl.multiple_of(h * HD, HD)
        return pltpu.make_async_copy(q_hbm.at[:, pl.ds(hc, HD)], qb.at[h], q_sem.at[h])

    d_copy = pltpu.make_async_copy(d_hbm, d_ref, small_sem.at[0])
    g_copy = pltpu.make_async_copy(g_hbm, g_ref, small_sem.at[1])
    owner_copy = pltpu.make_async_copy(owner_hbm, owner_ref, small_sem.at[2])
    idx_copy = pltpu.make_async_copy(idx_vec, idx_ref, small_sem.at[3])
    d_copy.start()
    owner_copy.start()

    def load(stage):
        @pl.loop(0, classes)
        def _(s):
            for copy in kv_copies(stage, s):
                copy.start()

    load(0)
    load(1)

    barrier = pltpu.get_barrier_semaphore()

    each_other(
        lambda j: pl.semaphore_signal(
            barrier, inc=1, device_id={"seq": j}, device_id_type=MESH
        )
    )
    for step in range(1, n_head):
        pl.semaphore_signal(
            barrier, inc=1, device_id={"head": lax.rem(z + step, n_head)}, device_id_type=MESH
        )

    d_copy.wait()
    lane = lax.broadcasted_iota(jnp.int32, (heads, 128), 1)
    start = whole = None
    for n in range(chunks):
        lo = n * CHUNK
        x0 = lanes_scan(d_ref[:, lo : lo + HALF] * LOG2E, lane)
        x1 = lanes_scan(d_ref[:, lo + HALF : lo + CHUNK] * LOG2E, lane)
        x1 = x1 + jnp.broadcast_to(x0[:, 127:128], (heads, 128))
        last = jnp.broadcast_to(x1[:, 127:128], (heads, 128))
        factors = jnp.exp2(last)
        decays = jnp.exp2(last - x0), jnp.exp2(last - x1)
        if n == 0:
            whole = jnp.zeros_like(last)
        if n % per_page == 0:
            start = jnp.zeros_like(last)
        begins, begins2 = jnp.exp2(start), jnp.exp2(whole)
        start, whole = start + last, whole + last
        pages = jnp.exp2(start)
        for h in range(heads):
            row = slice(h, h + 1)
            c_ref[h, :, lo : lo + HALF] = x0[row]
            c_ref[h, :, lo + HALF : lo + CHUNK] = x1[row]
            f_ref[h, :, lo : lo + HALF] = decays[0][row]
            f_ref[h, :, lo + HALF : lo + CHUNK] = decays[1][row]
            a_ref[h * chunks + n] = factors[row]
            b_ref[h * chunks + n] = begins[row]
            b2_ref[h * chunks + n] = begins2[row]
            if n % per_page == per_page - 1:
                pd_ref[h % classes, h // classes, n // per_page] = pages[row]

    def send_decays(j):
        return pltpu.make_async_remote_copy(
            src_ref=pd_ref.at[class_of(j)],
            dst_ref=dec_recv.at[me],
            send_sem=d_send,
            recv_sem=d_recv,
            device_id={"seq": j},
            device_id_type=MESH,
        )

    dec_recv[me] = pd_ref[mine]

    def send_rows(stage, j):
        return pltpu.make_async_remote_copy(
            src_ref=sendbuf.at[stage, j],
            dst_ref=recvbuf.at[stage, me],
            send_sem=a_send.at[stage],
            recv_sem=a_recv.at[stage],
            device_id={"seq": j},
            device_id_type=MESH,
        )

    def send_class(stage, cls):
        @pl.loop(0, 4)
        def _(a):
            for side in range(2):
                j = keeper(cls, lax.rem(x + far_first(a), 4), side)

                @pl.when(j != me)
                def _():
                    send_rows(stage, j).start()

                @pl.when(j == me)
                def _():
                    recvbuf[stage, me] = sendbuf[stage, me]

    def states(stage):
        @pl.loop(0, classes)
        def _(s):
            cls = class_at(s)
            h = stage * classes + cls
            for copy in kv_copies(stage, s):
                copy.wait()
            ends = []
            state = None
            for n in range(chunks):
                lo = n * CHUNK
                kt = kb[h, lo : lo + CHUNK, :].T
                scaled = (kt.astype(F32) * f_ref[h, :, lo : lo + CHUNK]).astype(BF)
                update = jnp.dot(scaled, vb[h, lo : lo + CHUNK, :], preferred_element_type=F32)
                if n == 0:
                    sl[h * chunks] = jnp.zeros_like(update, BF)
                elif n < per_page:
                    sl[h * chunks + n] = state.astype(BF)
                elif n == per_page:
                    sl[h * chunks + n] = ends[0].astype(BF)
                else:
                    sl[h * chunks + n] = (state + b_ref[h * chunks + n] * ends[0]).astype(BF)
                state = update if n % per_page == 0 else a_ref[h * chunks + n] * state + update
                if n % per_page == per_page - 1:
                    ends.append(state)
            for part in range(parts):
                j = keeper(cls, part // 2, part % 2)
                for page in range(2):
                    sendbuf[stage, j, page] = ends[page][part * rows : (part + 1) * rows].astype(BF)

            if stage > 0:
                send_class(stage, cls)

    tri = lax.broadcasted_iota(jnp.int32, (HALF, HALF), 0) >= lax.broadcasted_iota(
        jnp.int32, (HALF, HALF), 1
    )

    def intra(h):
        q_copy(h).wait()
        for n in range(chunks):
            lo = n * CHUNK
            q = qb[h, lo : lo + CHUNK, :]
            k = kb[h, lo : lo + CHUNK, :]
            row0 = c_ref[h, :, lo : lo + HALF]
            row1 = c_ref[h, :, lo + HALF : lo + CHUNK]
            col0, col1 = column_of(row0), column_of(row1)
            scores = lax.dot_general(
                q, k, (((1,), (1,)), ((), ())), preferred_element_type=F32
            )
            w00 = scores[:HALF, :HALF] * jnp.exp2(jnp.where(tri, col0 - row0, -1e30))
            w10 = scores[HALF:, :HALF] * jnp.exp2(col1 - row0)
            w11 = scores[HALF:, HALF:] * jnp.exp2(jnp.where(tri, col1 - row1, -1e30))
            out0 = jnp.dot(w00.astype(BF), vb[h, lo : lo + HALF, :], preferred_element_type=F32)
            out1 = jnp.dot(
                jnp.concatenate([w10.astype(BF), w11.astype(BF)], axis=1),
                vb[h, lo : lo + CHUNK, :],
                preferred_element_type=F32,
            )
            e0, e1 = jnp.exp2(col0), jnp.exp2(col1)
            if n > 0:
                carried = jnp.dot(q, sl[h * chunks + n], preferred_element_type=F32)
                out0 = out0 + e0 * carried[:HALF]
                out1 = out1 + e1 * carried[HALF:]
            acc[h, lo : lo + HALF, :] = out0
            acc[h, lo + HALF : lo + CHUNK, :] = out1
            ec[h, lo : lo + HALF, :] = e0
            ec[h, lo + HALF : lo + CHUNK, :] = e1

    def wait_rows(stage):
        arrived = recvbuf.at[stage, pl.ds(0, n_seq - 1)]
        pltpu.make_async_copy(arrived, arrived, a_recv.at[stage]).wait()

    def recur(stage):
        snap[0, stage] = jnp.zeros((rows, HD), BF)

        def pages_of(i, state):
            state = dec_recv[i, stage, 0] * state + recvbuf[stage, i, 0].astype(F32)
            snap[2 * i + 1, stage] = state.astype(BF)
            state = dec_recv[i, stage, 1] * state + recvbuf[stage, i, 1].astype(F32)
            snap[2 * i + 2, stage] = state.astype(BF)
            return state

        lax.fori_loop(0, n_seq, pages_of, jnp.zeros((rows, HD), F32), unroll=8)

    def send_entry(i):
        return pltpu.make_async_remote_copy(
            src_ref=snap.at[2 * i],
            dst_ref=ent.at[:, mine, pl.ds(r0, rows), :],
            send_sem=e_send,
            recv_sem=e_recv,
            device_id={"seq": i},
            device_id_type=MESH,
        )

    def kept(stage):
        return cache_hbm.at[:, stage * classes + mine, pl.ds(r0, rows), :]

    def send_pages(stage, i):
        return pltpu.make_async_remote_copy(
            src_ref=pagebuf.at[stage, pl.ds(i * SLOTS, SLOTS)],
            dst_ref=kept(stage),
            send_sem=p_send.at[stage],
            recv_sem=p_recv.at[stage],
            device_id={"seq": i},
            device_id_type=MESH,
        )

    def own_pages(stage):
        return pltpu.make_async_copy(
            pagebuf.at[stage, pl.ds(me * SLOTS, SLOTS)], kept(stage), p_self.at[stage]
        )

    def hand_out(stage):
        def fill(i):
            for s in range(SLOTS):
                pagebuf[stage, i * SLOTS + s] = snap[idx_ref[0, i * SLOTS + s], stage]

        def visit(i):
            fill(i)
            send_pages(stage, i).start()

        each_other(visit)
        fill(me)
        own_pages(stage).start()

    owner_copy.wait()
    n_pages = owner_ref.shape[1]
    square = (n_pages, n_pages)
    above = lax.broadcasted_iota(jnp.int32, square, 0)
    across = lax.broadcasted_iota(jnp.int32, square, 1)

    def turned(row):
        spread = jnp.broadcast_to(row, square)
        return jnp.max(jnp.where(above == across, spread, 0), axis=1, keepdims=True)

    owner = owner_ref[...]
    same = (turned(owner) == owner) & (above < across)
    slot = jnp.sum(jnp.where(same, 1, 0), axis=0, keepdims=True)
    target = turned(owner * SLOTS + slot)
    wide = (n_pages, 256)
    page = lax.broadcasted_iota(jnp.int32, wide, 0)
    place = lax.broadcasted_iota(jnp.int32, wide, 1)
    found = jnp.where(target == place, page + 1, 0)
    idx_vec[...] = jnp.max(found, axis=0, keepdims=True)
    idx_copy.start()

    states(0)
    pl.semaphore_wait(barrier, n_seq - 1 + n_head - 1)
    each_other(lambda j: send_decays(j).start())
    each_other(lambda j: send_rows(0, j).start())
    recvbuf[0, me] = sendbuf[0, me]

    @pl.loop(0, heads)
    def _(h):
        q_copy(h).start()

    g_copy.start()
    states(1)
    pl.loop(0, FIRST)(intra)
    all_decays = dec_recv.at[pl.ds(0, n_seq - 1)]
    pltpu.make_async_copy(all_decays, all_decays, d_recv).wait()
    idx_copy.wait()
    wait_rows(0)
    recur(0)
    pl.loop(FIRST, SECOND)(intra)
    wait_rows(1)
    recur(1)
    each_other(lambda i: send_entry(i).start())
    ent[:, mine, pl.ds(r0, rows), :] = snap[2 * me]

    hand_out(0)
    hand_out(1)
    pl.loop(SECOND, heads)(intra)

    entries = snap.at[pl.ds(0, n_seq - 1)]
    pltpu.make_async_copy(entries, entries, e_recv).wait()

    def send_squares(half, step):
        return pltpu.make_async_remote_copy(
            src_ref=sq_send.at[half],
            dst_ref=sq_recv.at[half, step - 1],
            send_sem=s_send.at[half],
            recv_sem=s_recv.at[half],
            device_id={"head": lax.rem(z + step, n_head)},
            device_id_type=MESH,
        )

    def finish(half):
        @pl.loop(0, per_page)
        def _(m):
            n = half * per_page + m
            lo = pl.multiple_of(n * CHUNK, CHUNK)
            squares = None
            for h in range(heads):
                carried = jnp.dot(
                    qb[h, pl.ds(lo, CHUNK), :],
                    ent[h // classes, h % classes],
                    preferred_element_type=F32,
                )
                scale = ec[h, pl.ds(lo, CHUNK), :] * b2_ref[h * chunks + n]
                out = acc[h, pl.ds(lo, CHUNK), :] + scale * carried
                acc[h, pl.ds(lo, CHUNK), :] = out
                squares = out * out if squares is None else squares + out * out
            sq_send[half, 2 * m] = jnp.sum(squares[:HALF].T, axis=0, keepdims=True)
            sq_send[half, 2 * m + 1] = jnp.sum(squares[HALF:].T, axis=0, keepdims=True)

        for step in range(1, n_head):
            send_squares(half, step).start()

    def out_copy(n):
        lo = pl.multiple_of(n * CHUNK, CHUNK)
        return pltpu.make_async_copy(
            ob.at[pl.ds(lo, CHUNK), :], att_hbm.at[pl.ds(lo, CHUNK), :], o_sem
        )

    def normalize(half):
        received = sq_recv.at[half]
        pltpu.make_async_copy(received, received, s_recv.at[half]).wait()
        total = sq_send[half]
        for step in range(n_head - 1):
            total = total + sq_recv[half, step]
        scale_ref[...] = lax.rsqrt(total / (heads * HD * n_head) + 1e-6)

        @pl.loop(0, per_page)
        def _(m):
            n = half * per_page + m
            lo = pl.multiple_of(n * CHUNK, CHUNK)
            for side in range(2):
                scale = column_of(scale_ref[2 * m + side])
                at = pl.ds(pl.multiple_of(lo + side * HALF, HALF), HALF)
                for h in range(heads):
                    ob[at, h * HD : (h + 1) * HD] = (
                        acc[h, at, :] * scale * g_ref[h : h + 1, :]
                    ).astype(BF)
            out_copy(n).start()

    finish(0)
    finish(1)
    g_copy.wait()
    normalize(0)
    normalize(1)

    pltpu.make_async_copy(entries, entries, e_send).wait()
    pltpu.make_async_copy(ob, att_hbm, o_sem).wait()
    pltpu.make_async_copy(all_decays, all_decays, d_send).wait()
    for half in range(2):
        received = sq_recv.at[half]
        pltpu.make_async_copy(received, received, s_send.at[half]).wait()
    for stage in range(STAGES):
        sent = sendbuf.at[stage, pl.ds(0, n_seq - 1)]
        pltpu.make_async_copy(sent, sent, a_send.at[stage]).wait()
        own_pages(stage).wait()
        pages = pagebuf.at[stage, pl.ds(0, (n_seq - 1) * SLOTS)]
        pltpu.make_async_copy(pages, pages, p_send.at[stage]).wait()
        pltpu.make_async_copy(pages, pages, p_recv.at[stage]).wait()


def shards(n_seq, n_head, queries, key_rows, value_rows, decay_log, norm_gain, page_owner):
    toks, width = queries.shape
    heads = decay_log.shape[0]
    chunks = toks // CHUNK
    classes = heads // STAGES
    rows = HD * classes // n_seq
    n_pages = page_owner.shape[0]
    anywhere = pl.BlockSpec(memory_space=pl.ANY)
    dma = pltpu.SemaphoreType.DMA
    return pl.pallas_call(
        functools.partial(kernel, n_seq, n_head),
        out_shape=(
            jax.ShapeDtypeStruct((toks, width), BF),
            jax.ShapeDtypeStruct((SLOTS, heads, HD, HD), BF),
        ),
        in_specs=[pl.BlockSpec(memory_space=pltpu.HBM)] * 6,
        out_specs=(anywhere, anywhere),
        scratch_shapes=[
            pltpu.VMEM((heads, toks, HD), BF),
            pltpu.VMEM((heads, toks, HD), BF),
            pltpu.VMEM((heads, toks, HD), BF),
            pltpu.VMEM((heads, toks, HD), F32),
            pltpu.VMEM((heads, toks, HD), F32),
            pltpu.VMEM((toks, width), BF),
            pltpu.VMEM((heads * chunks, HD, HD), BF),
            pltpu.VMEM((heads, toks), F32),
            pltpu.VMEM((heads, HD), F32),
            pltpu.VMEM((1, n_pages), jnp.int32),
            pltpu.VMEM((1, 256), jnp.int32),
            pltpu.SMEM((1, 256), jnp.int32),
            pltpu.VMEM((heads, 1, toks), F32),
            pltpu.VMEM((heads, 1, toks), F32),
            pltpu.VMEM((heads * chunks, 1, 128), F32),
            pltpu.VMEM((heads * chunks, 1, 128), F32),
            pltpu.VMEM((heads * chunks, 1, 128), F32),
            pltpu.VMEM((classes, STAGES, 2, 1, 128), F32),
            pltpu.VMEM((n_seq, STAGES, 2, 1, 128), F32),
            pltpu.VMEM((STAGES, n_seq, 2, rows, HD), BF),
            pltpu.VMEM((STAGES, n_seq, 2, rows, HD), BF),
            pltpu.VMEM((n_pages + 1, STAGES, rows, HD), BF),
            pltpu.VMEM((STAGES, n_seq * SLOTS, rows, HD), BF),
            pltpu.VMEM((STAGES, classes, HD, HD), BF),
            pltpu.VMEM((2, 8, 1, 128), F32),
            pltpu.VMEM((2, n_head - 1, 8, 1, 128), F32),
            pltpu.VMEM((8, 1, 128), F32),
            dma((2, heads)),
            dma((heads,)),
            dma((4,)),
            dma,
            dma,
            dma((STAGES,)),
            dma((STAGES,)),
            dma,
            dma,
            dma((STAGES,)),
            dma((STAGES,)),
            dma((STAGES,)),
            dma((2,)),
            dma((2,)),
            dma,
        ],
        compiler_params=pltpu.CompilerParams(
            collective_id=0, has_side_effects=True, vmem_limit_bytes=48 * 1024 * 1024
        ),
    )(
        queries,
        key_rows,
        value_rows,
        pltpu.with_memory_space_constraint(decay_log, pltpu.HBM),
        pltpu.with_memory_space_constraint(norm_gain.reshape(heads, HD), pltpu.HBM),
        pltpu.with_memory_space_constraint(page_owner.reshape(1, n_pages), pltpu.HBM),
    )


def solution(mesh):
    return jax.shard_map(
        functools.partial(shards, mesh.shape["seq"], mesh.shape["head"]),
        mesh=mesh,
        in_specs=(
            P("seq", "head"),
            P("seq", "head"),
            P("seq", "head"),
            P("head", "seq"),
            P("head"),
            P(),
        ),
        out_specs=(P("seq", "head"), P("seq", "head", None, None)),
        check_vma=False,
    )
```
